32 devices in a mesh: energy: 2 (over y), slab: 4 (over z), col: 2 (over x), orb: 2 (over core).
Axes of the slice: x: 2, y: 2, z: 4, core: 2. Of those that a mesh axis runs over, the one named last changes fastest.
Arguments:
- rhs: bfloat16 [2, 8, 512, 1024], P(None, ('energy', 'slab'), None, ('col', 'orb')), parts along dimension 1, may hold values from -6 to 6
- dinv: bfloat16 [2, 8, 512, 512], P(None, ('energy', 'slab'), 'orb'), parts along dimension 1, may hold values from -0.078125 to 1.125
- spikes: bfloat16 [2, 8, 2, 512, 512], P(None, ('energy', 'slab'), None, 'orb'), parts along dimension 1, may hold values from -0.09375 to 0.09375
- merge_inv: bfloat16 [2, 8, 512, 512], P(None, ('energy', 'slab'), 'orb'), parts along dimension 1, may hold values from -0.078125 to 1.125
Outputs:
- solution: float32 [2, 8, 512, 1024], P(None, ('energy', 'slab'), None, ('col', 'orb')), parts along dimension 1
The draws below stay inside these ranges and needn't reach their ends.
There are 2 independent parts, one for each index of `energy`. The reference program is written for one: setup_inputs(seed, part) draws one part's arguments, and reference() takes and returns one part's arrays. A program takes and returns all parts, laid end to end along the dimension named above; each array names one. Nothing has to cross between parts.
All inputs are finite; a program needn't handle non-finite values.
Results may differ from the reference program's by a relative error of at most 0.013.
Values may be sent and summed in bfloat16 or wider, within the bound.
A program may use at most 64 MiB of HBM per device.

```python
import jax
import jax.numpy as jnp

ORBS = 512
COLS = 1024
SLICES = 4
LEVELS = 2


def identity_blocks(key):
    noise_key = jax.random.fold_in(key, 1)
    diag_key = jax.random.fold_in(key, 2)
    noise = jnp.clip(jax.random.normal(noise_key, (2, SLICES, ORBS, ORBS), jnp.float32), -4.0, 4.0)
    noise = noise / -jnp.min(noise) * 0.078125
    unit_matrix = jnp.eye(ORBS, dtype=jnp.float32)
    raw_diag = jax.random.uniform(diag_key, (SLICES, ORBS), jnp.float32, 0.0, 1.0)
    lowest = jnp.min(raw_diag)
    highest = jnp.max(raw_diag)
    shifted = (raw_diag - lowest) / (highest - lowest)
    diag_part = 0.125 * (2.0 * shifted - 1.0)
    real_part = noise[0] * (1.0 - unit_matrix) + unit_matrix * (1.0 + diag_part[:, :, None])
    return jnp.stack([real_part, noise[1]]).astype(jnp.bfloat16)


def draw_dinv(key, part):
    return identity_blocks(jax.random.fold_in(key, 11))


def draw_merge_inv(key, part):
    return identity_blocks(jax.random.fold_in(key, 23))


def block_scale(key, dims, shards, smallest, high):
    level, own = 1.0, jax.random.fold_in(key, 6)
    for dim, parts in shards:
        draws = jnp.exp(jax.random.uniform(jax.random.fold_in(own, dim), (parts,), jnp.float32, smallest / len(shards), high / len(shards)))
        level = level * jnp.repeat(draws, dims[dim] // parts).reshape([-1 if axis == dim else 1 for axis in range(len(dims))])
    return level


def centred(key, extent, scale, reach, shards=(), held_as=jnp.bfloat16):
    values = jax.random.normal(key, extent, jnp.float32) * scale
    if len(shards) > 0:
        values = block_scale(key, extent, shards, -0.22, 0.18) * values
    return jnp.clip(values, min=-reach, max=reach).astype(held_as)


def setup_inputs(seed: int = 0, part: int = 0) -> dict:
    arg_keys = jax.random.split(jax.random.key(seed), 5)
    part_keys = jax.random.split(jax.random.fold_in(arg_keys[4], part), 5)
    rhs = centred(part_keys[0], (2, SLICES, ORBS, COLS), 1.0, 6.0, ((1, 4), (3, 4)))
    dinv = draw_dinv(jax.random.fold_in(jax.random.fold_in(arg_keys[4], part), 71), part)
    spikes = centred(part_keys[2], (2, SLICES, LEVELS, ORBS, ORBS), (8 * ORBS) ** -0.5, 0.09375, ((1, 4), (3, 2)))
    merge_inv = draw_merge_inv(jax.random.fold_in(jax.random.fold_in(arg_keys[4], part), 71), part)
    return {"rhs": rhs, "dinv": dinv, "spikes": spikes, "merge_inv": merge_inv}


def complex_product(matrix, operand):
    matrix = matrix.astype(jnp.float32)
    operand = operand.astype(jnp.float32)
    real_part = jnp.einsum("...ij,...jk->...ik", matrix[0], operand[0]) - jnp.einsum("...ij,...jk->...ik", matrix[1], operand[1])
    imag_part = jnp.einsum("...ij,...jk->...ik", matrix[0], operand[1]) + jnp.einsum("...ij,...jk->...ik", matrix[1], operand[0])
    return jnp.stack([real_part, imag_part])


def reference(rhs, dinv, spikes, merge_inv):
    current = complex_product(dinv, rhs)
    for height in range(LEVELS):
        half_span = 2 ** height
        groups = SLICES // (2 * half_span)
        shaped = current.reshape(2, groups, 2 * half_span, ORBS, COLS)
        rounded = shaped.astype(jnp.bfloat16)
        spike_now = spikes[:, :, height].reshape(2, groups, 2 * half_span, ORBS, ORBS)
        merge_now = merge_inv.reshape(2, groups, 2 * half_span, ORBS, ORBS)[:, :, half_span - 1]
        interior = shaped[:, :, half_span - 1] - complex_product(spike_now[:, :, half_span - 1], rounded[:, :, half_span])
        left_tip = complex_product(merge_now, interior.astype(jnp.bfloat16)).astype(jnp.bfloat16)
        spread_left = jnp.broadcast_to(left_tip[:, :, None], (2, groups, half_span, ORBS, COLS))
        right_part = shaped[:, :, half_span:] - complex_product(spike_now[:, :, half_span:], spread_left)
        right_tip = right_part[:, :, 0].astype(jnp.bfloat16)
        spread_right = jnp.broadcast_to(right_tip[:, :, None], (2, groups, half_span, ORBS, COLS))
        left_part = shaped[:, :, :half_span] - complex_product(spike_now[:, :, :half_span], spread_right)
        current = jnp.concatenate([left_part, right_part], axis=2).reshape(2, SLICES, ORBS, COLS)
    return current
```

```python
import functools

import jax
import jax.numpy as jnp
from jax import lax
from jax.experimental import pallas as pl
from jax.experimental.pallas import tpu as pltpu
from jax.sharding import PartitionSpec as P

MESH = pl.DeviceIdType.MESH


def kernel(
    slabs,
    rhs_ref,
    dinv_ref,
    spikes_ref,
    merge_ref,
    out_ref,
    dfull,
    sfull,
    mfull,
    pown,
    pbuf,
    vbuf,
    xbuf,
    hbuf,
    ybuf,
    ibuf,
    tbuf,
    zbuf,
    tips,
    local_sem,
    orb_send,
    orb_recv,
    mat_send,
    mat_recv,
    ex_send,
    fw_send,
    tip_recv,
):
    s = lax.axis_index("slab")
    o = lax.axis_index("orb")
    levels = sfull.shape[1]
    orbs = dfull.shape[1]
    half = dinv_ref.shape[2]
    chunks = xbuf.shape[0]
    cw = xbuf.shape[2] // 2
    rb = 256
    has_up = s < slabs - 1
    has_down = s > 0
    up = {"slab": s + 1}
    down = {"slab": s - 1}
    other = {"orb": 1 - o}
    mine = pl.ds(pl.multiple_of(o * half, half), half)

    left_level = jnp.int32(0)
    right_level = jnp.int32(0)
    for l in range(levels):
        span = 1 << l
        pos = lax.rem(s, 2 * span)
        left_level = jnp.where(pos == span - 1, l, left_level)
        right_level = jnp.where(pos == span, l, right_level)

    def remote(src, dst, send, recv, to):
        return pltpu.make_async_remote_copy(
            src_ref=src, dst_ref=dst, send_sem=send, recv_sem=recv, device_id=to, device_id_type=MESH
        )

    def when(cond, fn):
        pl.when(cond)(fn)

    parts = (
        (spikes_ref.at[:, 0], sfull.at[:, :, mine]),
        (dinv_ref.at[:, 0], dfull.at[:, mine]),
        (merge_ref.at[:, 0], mfull.at[:, mine]),
    )
    own = [pltpu.make_async_copy(a, b, local_sem.at[k]) for k, (a, b) in enumerate(parts)]
    for copy in own:
        copy.start()
    barrier = pltpu.get_barrier_semaphore()
    pl.semaphore_signal(barrier, inc=1, device_id=other, device_id_type=MESH)
    when(has_up, lambda: pl.semaphore_signal(barrier, inc=1, device_id=up, device_id_type=MESH))
    when(has_down, lambda: pl.semaphore_signal(barrier, inc=1, device_id=down, device_id_type=MESH))
    pl.semaphore_wait(barrier, 1 + jnp.where(has_up, 1, 0) + jnp.where(has_down, 1, 0))

    swaps = [remote(a, b, orb_send.at[k], orb_recv.at[k], other) for k, (a, b) in enumerate(parts)]
    for copy in swaps:
        copy.start()
    send_v = remote(spikes_ref.at[:, 0, right_level], vbuf.at[:, mine], mat_send.at[0], mat_recv.at[0], down)
    send_p = remote(pown, pbuf.at[:, mine], mat_send.at[1], mat_recv.at[1], up)
    pass_v = remote(vbuf.at[:, mine], vbuf.at[:, mine], mat_send.at[2], mat_recv.at[2], other)
    pass_p = remote(pbuf.at[:, mine], pbuf.at[:, mine], mat_send.at[3], mat_recv.at[3], other)
    when(has_down, send_v.start)

    def product(mat, x, emit):
        def body(r, carry):
            rows = pl.ds(pl.multiple_of(r * rb, rb), rb)
            a = jnp.dot(mat[0, rows, :], x[...], preferred_element_type=jnp.float32)
            b = jnp.dot(mat[1, rows, :], x[...], preferred_element_type=jnp.float32)
            emit(rows, a[:, :cw] - b[:, cw:], a[:, cw:] + b[:, :cw])
            return carry

        lax.fori_loop(0, orbs // rb, body, 0)

    own[0].wait()
    swaps[0].wait_recv()

    @pl.when(has_up)
    def _():
        def body(j, carry):
            cols = pl.ds(pl.multiple_of(j * rb, rb), rb)
            re = sfull[0, left_level, :, cols]
            im = sfull[1, left_level, :, cols]
            m0 = merge_ref[0, 0]
            m1 = merge_ref[1, 0]
            dot = functools.partial(jnp.dot, preferred_element_type=jnp.float32)
            pown[0, :, cols] = (dot(m0, re) - dot(m1, im)).astype(jnp.bfloat16)
            pown[1, :, cols] = (dot(m0, im) + dot(m1, re)).astype(jnp.bfloat16)
            return carry

        lax.fori_loop(0, orbs // rb, body, 0)
        send_p.start()

    own[1].wait()
    swaps[1].wait_recv()
    own[2].wait()
    swaps[2].wait_recv()

    def roles(l):
        span = 1 << l
        pos = lax.rem(s, 2 * span)
        return span, pos, pos == span - 1, pos == span

    def exchange_copies(l, c):
        send = ex_send.at[l, c]
        recv = tip_recv.at[l, c]
        return (
            remote(ybuf.at[c], tips.at[l, c], send, recv, up),
            remote(hbuf.at[l, c], tips.at[l, c], send, recv, down),
        )

    def forward_copies(l, c):
        span, pos, is_left, is_right = roles(l)
        send = fw_send.at[l, c]
        recv = tip_recv.at[l, c]
        out = []
        if span > 1:
            out = [
                (is_left, remote(zbuf.at[l, c], tips.at[l, c], send, recv, down)),
                (is_right, remote(zbuf.at[l, c], tips.at[l, c], send, recv, up)),
                ((pos > 0) & (pos < span - 1), remote(tips.at[l, c], tips.at[l, c], send, recv, down)),
                ((pos > span) & (pos < 2 * span - 1), remote(tips.at[l, c], tips.at[l, c], send, recv, up)),
            ]
        return out

    def offer(l, c):
        span, pos, is_left, is_right = roles(l)
        to_right, to_left = exchange_copies(l, c)

        @pl.when(is_right)
        def _():
            to_left.start()

        @pl.when(is_left)
        def _():
            def emit(rows, re, im):
                ybuf[c, rows, :cw] = re.astype(jnp.bfloat16)
                ybuf[c, rows, cw:] = im.astype(jnp.bfloat16)

            product(mfull, hbuf.at[l, c], emit)
            to_right.start()

    def settle(l, c):
        span, pos, is_left, is_right = roles(l)
        cols = pl.ds(c * cw, cw)
        spike = sfull.at[:, l]
        tip = tips.at[l, c]
        forwards = forward_copies(l, c)
        exchange_copies(l, c)[0].wait_recv()
        if span > 1:
            for cond, copy in forwards[2:]:
                when(cond, copy.start)

        @pl.when(is_right)
        def _():
            def emit(rows, re, im):
                zbuf[l, c, rows, :cw] = (tip[rows, :cw].astype(jnp.float32) - re).astype(jnp.bfloat16)
                zbuf[l, c, rows, cw:] = (tip[rows, cw:].astype(jnp.float32) - im).astype(jnp.bfloat16)

            product(pbuf, hbuf.at[l, c], emit)
            if span > 1:
                forwards[1][1].start()

        @pl.when(is_left)
        def _():
            def emit_interior(rows, re, im):
                ibuf[rows, :cw] = (out_ref[0, 0, rows, cols] - re).astype(jnp.bfloat16)
                ibuf[rows, cw:] = (out_ref[1, 0, rows, cols] - im).astype(jnp.bfloat16)

            def emit_left(rows, re, im):
                tbuf[rows, :cw] = re.astype(jnp.bfloat16)
                tbuf[rows, cw:] = im.astype(jnp.bfloat16)

            def emit_right(rows, re, im):
                zbuf[l, c, rows, :cw] = (tip[rows, :cw].astype(jnp.float32) - re).astype(jnp.bfloat16)
                zbuf[l, c, rows, cw:] = (tip[rows, cw:].astype(jnp.float32) - im).astype(jnp.bfloat16)

            product(spike, tip, emit_interior)
            product(mfull, ibuf, emit_left)
            product(vbuf, tbuf, emit_right)
            if span > 1:
                forwards[0][1].start()

        def update(z):
            def emit(rows, re, im):
                re = out_ref[0, 0, rows, cols] - re
                im = out_ref[1, 0, rows, cols] - im
                out_ref[0, 0, rows, cols] = re
                out_ref[1, 0, rows, cols] = im
                if l + 1 < levels:
                    hbuf[l + 1, c, rows, :cw] = re.astype(jnp.bfloat16)
                    hbuf[l + 1, c, rows, cw:] = im.astype(jnp.bfloat16)

            product(spike, z, emit)

        if span == 1:
            update(zbuf.at[l, c])
        else:
            interface = is_left | is_right
            when(interface, lambda: update(zbuf.at[l, c]))
            when(jnp.logical_not(interface), lambda: update(tip))

    for c in range(chunks):
        cols = pl.ds(c * cw, cw)
        xbuf[c, :, :cw] = rhs_ref[0, 0, :, cols]
        xbuf[c, :, cw:] = rhs_ref[1, 0, :, cols]

        def emit(rows, re, im, c=c, cols=cols):
            out_ref[0, 0, rows, cols] = re
            out_ref[1, 0, rows, cols] = im
            hbuf[0, c, rows, :cw] = re.astype(jnp.bfloat16)
            hbuf[0, c, rows, cw:] = im.astype(jnp.bfloat16)

        product(dfull, xbuf.at[c], emit)
        offer(0, c)

    @pl.when(has_up)
    def _():
        send_v.wait_recv()
        pass_v.start()

    @pl.when(has_down)
    def _():
        send_p.wait_recv()
        pass_p.start()

    when(has_up, pass_v.wait_recv)
    when(has_down, pass_p.wait_recv)

    for l in range(levels):
        for c in range(chunks):
            settle(l, c)
            if l + 1 < levels:
                offer(l + 1, c)

    for copy in swaps:
        copy.wait_send()
    when(has_down, send_v.wait_send)
    when(has_up, send_p.wait_send)
    when(has_up, pass_v.wait_send)
    when(has_down, pass_p.wait_send)
    for l in range(levels):
        span, pos, is_left, is_right = roles(l)
        for c in range(chunks):
            to_right, to_left = exchange_copies(l, c)
            when(is_left, to_right.wait_send)
            when(is_right, to_left.wait_send)
            for cond, copy in forward_copies(l, c):
                when(cond, copy.wait_send)


def per_device(slabs, rhs, dinv, spikes, merge_inv):
    _, _, orbs, width = rhs.shape
    half = dinv.shape[2]
    levels = spikes.shape[2]
    cw = min(128, width)
    chunks = width // cw
    bf16 = jnp.bfloat16
    vm = pltpu.VMEM
    dma = pltpu.SemaphoreType.DMA
    return pl.pallas_call(
        functools.partial(kernel, slabs),
        out_shape=jax.ShapeDtypeStruct(rhs.shape, jnp.float32),
        in_specs=[pl.BlockSpec(memory_space=pltpu.VMEM)] * 4,
        out_specs=pl.BlockSpec(memory_space=pltpu.VMEM),
        scratch_shapes=[
            vm((2, orbs, orbs), bf16),
            vm((2, levels, orbs, orbs), bf16),
            vm((2, orbs, orbs), bf16),
            vm((2, half, orbs), bf16),
            vm((2, orbs, orbs), bf16),
            vm((2, orbs, orbs), bf16),
            vm((chunks, orbs, 2 * cw), bf16),
            vm((levels, chunks, orbs, 2 * cw), bf16),
            vm((chunks, orbs, 2 * cw), bf16),
            vm((orbs, 2 * cw), bf16),
            vm((orbs, 2 * cw), bf16),
            vm((levels, chunks, orbs, 2 * cw), bf16),
            vm((levels, chunks, orbs, 2 * cw), bf16),
            dma((3,)),
            dma((3,)),
            dma((3,)),
            dma((4,)),
            dma((4,)),
            dma((levels, chunks)),
            dma((levels, chunks)),
            dma((levels, chunks)),
        ],
        compiler_params=pltpu.CompilerParams(
            collective_id=0, has_side_effects=True, vmem_limit_bytes=56 * 1024 * 1024
        ),
    )(rhs, dinv, spikes, merge_inv)


def solution(mesh):
    placed = (
        P(None, ("energy", "slab"), None, ("col", "orb")),
        P(None, ("energy", "slab"), "orb", None),
        P(None, ("energy", "slab"), None, "orb", None),
        P(None, ("energy", "slab"), "orb", None),
    )
    return jax.shard_map(
        functools.partial(per_device, mesh.shape["slab"]),
        mesh=mesh,
        in_specs=placed,
        out_specs=P(None, ("energy", "slab"), None, ("col", "orb")),
        check_vma=False,
    )
```

```python
import functools

import jax
import jax.numpy as jnp
from jax import lax
from jax.experimental import pallas as pl
from jax.experimental.pallas import tpu as pltpu
from jax.sharding import PartitionSpec as P

MESH = pl.DeviceIdType.MESH


def kernel(
    slabs,
    cols_count,
    rhs_ref,
    dinv_ref,
    spikes_ref,
    merge_ref,
    out_ref,
    dfull,
    sfull,
    mfull,
    pown,
    pbuf,
    vbuf,
    xbuf,
    hbuf,
    ybuf,
    ibuf,
    tbuf,
    zbuf,
    tips,
    local_sem,
    orb_send,
    orb_recv,
    mat_send,
    mat_recv,
    share_send,
    share_recv,
    ex_send,
    fw_send,
    tip_recv,
):
    s = lax.axis_index("slab")
    o = lax.axis_index("orb")
    x = lax.axis_index("col")
    levels = sfull.shape[1]
    orbs = dfull.shape[1]
    half = dinv_ref.shape[2]
    chunks = xbuf.shape[0]
    cw = xbuf.shape[2] // 2
    rb = 256
    has_up = s < slabs - 1
    has_down = s > 0
    up = {"slab": s + 1}
    down = {"slab": s - 1}
    other = {"orb": 1 - o}
    mine = pl.ds(pl.multiple_of(o * half, half), half)
    piece = half // cols_count
    part = pl.ds(pl.multiple_of(x * piece, piece), piece)
    place = pl.ds(pl.multiple_of(o * half + x * piece, piece), piece)

    left_level = jnp.int32(0)
    right_level = jnp.int32(0)
    for l in range(levels):
        span = 1 << l
        pos = lax.rem(s, 2 * span)
        left_level = jnp.where(pos == span - 1, l, left_level)
        right_level = jnp.where(pos == span, l, right_level)

    def remote(src, dst, send, recv, to):
        return pltpu.make_async_remote_copy(
            src_ref=src, dst_ref=dst, send_sem=send, recv_sem=recv, device_id=to, device_id_type=MESH
        )

    def when(cond, fn):
        pl.when(cond)(fn)

    parts = [
        (spikes_ref.at[:, 0, left_level], sfull.at[:, left_level, mine]),
        (dinv_ref.at[:, 0], dfull.at[:, mine]),
        (merge_ref.at[:, 0], mfull.at[:, mine]),
    ]
    for k in range(1, levels):
        level = lax.rem(left_level + k, levels)
        parts.append((spikes_ref.at[:, 0, level], sfull.at[:, level, mine]))
    own = [pltpu.make_async_copy(a, b, local_sem.at[k]) for k, (a, b) in enumerate(parts)]
    for copy in own:
        copy.start()
    barrier = pltpu.get_barrier_semaphore()
    pl.semaphore_signal(barrier, inc=1, device_id=other, device_id_type=MESH)
    when(has_up, lambda: pl.semaphore_signal(barrier, inc=1, device_id=up, device_id_type=MESH))
    when(has_down, lambda: pl.semaphore_signal(barrier, inc=1, device_id=down, device_id_type=MESH))
    beside = [{"col": lax.rem(x + k, cols_count)} for k in range(1, cols_count)]
    for to in beside:
        pl.semaphore_signal(barrier, inc=1, device_id=to, device_id_type=MESH)
    pl.semaphore_wait(barrier, cols_count + jnp.where(has_up, 1, 0) + jnp.where(has_down, 1, 0))

    swaps = [remote(a, b, orb_send.at[k], orb_recv.at[k], other) for k, (a, b) in enumerate(parts)]
    for copy in swaps:
        copy.start()
    send_v = remote(spikes_ref.at[:, 0, right_level, part], vbuf.at[:, place], mat_send.at[0], mat_recv.at[0], down)
    send_p = remote(pown, pbuf.at[:, place], mat_send.at[1], mat_recv.at[1], up)
    share_v = [
        remote(vbuf.at[:, place], vbuf.at[:, place], share_send.at[0, k], share_recv.at[0, k], to)
        for k, to in enumerate(beside)
    ]
    share_p = [
        remote(pbuf.at[:, place], pbuf.at[:, place], share_send.at[1, k], share_recv.at[1, k], to)
        for k, to in enumerate(beside)
    ]
    pass_v = remote(vbuf.at[:, mine], vbuf.at[:, mine], mat_send.at[2], mat_recv.at[2], other)
    pass_p = remote(pbuf.at[:, mine], pbuf.at[:, mine], mat_send.at[3], mat_recv.at[3], other)
    when(has_down, send_v.start)

    def product(mat, x, emit):
        def body(r, carry):
            rows = pl.ds(pl.multiple_of(r * rb, rb), rb)
            a = jnp.dot(mat[0, rows, :], x[...], preferred_element_type=jnp.float32)
            b = jnp.dot(mat[1, rows, :], x[...], preferred_element_type=jnp.float32)
            emit(rows, a[:, :cw] - b[:, cw:], a[:, cw:] + b[:, :cw])
            return carry

        lax.fori_loop(0, orbs // rb, body, 0)

    own[0].wait()
    own[2].wait()
    swaps[0].wait_recv()

    @pl.when(has_up)
    def _():
        def body(j, carry):
            cols = pl.ds(pl.multiple_of(j * rb, rb), rb)
            re = sfull[0, left_level, :, cols]
            im = sfull[1, left_level, :, cols]
            m0 = mfull[0, place, :]
            m1 = mfull[1, place, :]
            dot = functools.partial(jnp.dot, preferred_element_type=jnp.float32)
            pown[0, :, cols] = (dot(m0, re) - dot(m1, im)).astype(jnp.bfloat16)
            pown[1, :, cols] = (dot(m0, im) + dot(m1, re)).astype(jnp.bfloat16)
            return carry

        lax.fori_loop(0, orbs // rb, body, 0)
        send_p.start()

    own[1].wait()
    swaps[1].wait_recv()
    swaps[2].wait_recv()

    def roles(l):
        span = 1 << l
        pos = lax.rem(s, 2 * span)
        return span, pos, pos == span - 1, pos == span

    def exchange_copies(l, c):
        send = ex_send.at[l, c]
        recv = tip_recv.at[l, c]
        return (
            remote(ybuf.at[c], tips.at[l, c], send, recv, up),
            remote(hbuf.at[l, c], tips.at[l, c], send, recv, down),
        )

    def forward_copies(l, c):
        span, pos, is_left, is_right = roles(l)
        send = fw_send.at[l, c]
        recv = tip_recv.at[l, c]
        out = []
        if span > 1:
            out = [
                (is_left, remote(zbuf.at[l, c], tips.at[l, c], send, recv, down)),
                (is_right, remote(zbuf.at[l, c], tips.at[l, c], send, recv, up)),
                ((pos > 0) & (pos < span - 1), remote(tips.at[l, c], tips.at[l, c], send, recv, down)),
                ((pos > span) & (pos < 2 * span - 1), remote(tips.at[l, c], tips.at[l, c], send, recv, up)),
            ]
        return out

    def offer(l, c):
        span, pos, is_left, is_right = roles(l)
        to_right, to_left = exchange_copies(l, c)

        @pl.when(is_right)
        def _():
            to_left.start()

        @pl.when(is_left)
        def _():
            def emit(rows, re, im):
                ybuf[c, rows, :cw] = re.astype(jnp.bfloat16)
                ybuf[c, rows, cw:] = im.astype(jnp.bfloat16)

            product(mfull, hbuf.at[l, c], emit)
            to_right.start()

    def settle(l, c):
        span, pos, is_left, is_right = roles(l)
        cols = pl.ds(c * cw, cw)
        spike = sfull.at[:, l]
        tip = tips.at[l, c]
        forwards = forward_copies(l, c)
        exchange_copies(l, c)[0].wait_recv()
        if span > 1:
            for cond, copy in forwards[2:]:
                when(cond, copy.start)

        @pl.when(is_right)
        def _():
            def emit(rows, re, im):
                zbuf[l, c, rows, :cw] = (tip[rows, :cw].astype(jnp.float32) - re).astype(jnp.bfloat16)
                zbuf[l, c, rows, cw:] = (tip[rows, cw:].astype(jnp.float32) - im).astype(jnp.bfloat16)

            product(pbuf, hbuf.at[l, c], emit)
            if span > 1:
                forwards[1][1].start()

        @pl.when(is_left)
        def _():
            def emit_interior(rows, re, im):
                ibuf[rows, :cw] = (out_ref[0, 0, rows, cols] - re).astype(jnp.bfloat16)
                ibuf[rows, cw:] = (out_ref[1, 0, rows, cols] - im).astype(jnp.bfloat16)

            def emit_left(rows, re, im):
                tbuf[rows, :cw] = re.astype(jnp.bfloat16)
                tbuf[rows, cw:] = im.astype(jnp.bfloat16)

            def emit_right(rows, re, im):
                zbuf[l, c, rows, :cw] = (tip[rows, :cw].astype(jnp.float32) - re).astype(jnp.bfloat16)
                zbuf[l, c, rows, cw:] = (tip[rows, cw:].astype(jnp.float32) - im).astype(jnp.bfloat16)

            product(spike, tip, emit_interior)
            product(mfull, ibuf, emit_left)
            product(vbuf, tbuf, emit_right)
            if span > 1:
                forwards[0][1].start()

        def update(z):
            def emit(rows, re, im):
                re = out_ref[0, 0, rows, cols] - re
                im = out_ref[1, 0, rows, cols] - im
                out_ref[0, 0, rows, cols] = re
                out_ref[1, 0, rows, cols] = im
                if l + 1 < levels:
                    hbuf[l + 1, c, rows, :cw] = re.astype(jnp.bfloat16)
                    hbuf[l + 1, c, rows, cw:] = im.astype(jnp.bfloat16)

            product(spike, z, emit)

        if span == 1:
            update(zbuf.at[l, c])
        else:
            interface = is_left | is_right
            when(interface, lambda: update(zbuf.at[l, c]))
            when(jnp.logical_not(interface), lambda: update(tip))

    for c in range(chunks):
        cols = pl.ds(c * cw, cw)
        xbuf[c, :, :cw] = rhs_ref[0, 0, :, cols]
        xbuf[c, :, cw:] = rhs_ref[1, 0, :, cols]

        def emit(rows, re, im, c=c, cols=cols):
            out_ref[0, 0, rows, cols] = re
            out_ref[1, 0, rows, cols] = im
            hbuf[0, c, rows, :cw] = re.astype(jnp.bfloat16)
            hbuf[0, c, rows, cw:] = im.astype(jnp.bfloat16)

        product(dfull, xbuf.at[c], emit)
        offer(0, c)

    def run(copies, name):
        def go():
            for copy in copies:
                getattr(copy, name)()

        return go

    for k in range(3, len(parts)):
        own[k].wait()
        swaps[k].wait_recv()

    @pl.when(has_up)
    def _():
        send_v.wait_recv()
        run(share_v, "start")()

    @pl.when(has_down)
    def _():
        send_p.wait_recv()
        run(share_p, "start")()

    @pl.when(has_up)
    def _():
        run(share_v, "wait_recv")()
        pass_v.start()

    @pl.when(has_down)
    def _():
        run(share_p, "wait_recv")()
        pass_p.start()

    when(has_up, pass_v.wait_recv)
    when(has_down, pass_p.wait_recv)

    for l in range(levels):
        for c in range(chunks):
            settle(l, c)
            if l + 1 < levels:
                offer(l + 1, c)

    for copy in swaps:
        copy.wait_send()
    when(has_down, send_v.wait_send)
    when(has_up, send_p.wait_send)
    when(has_up, run(share_v, "wait_send"))
    when(has_down, run(share_p, "wait_send"))
    when(has_up, pass_v.wait_send)
    when(has_down, pass_p.wait_send)
    for l in range(levels):
        span, pos, is_left, is_right = roles(l)
        for c in range(chunks):
            to_right, to_left = exchange_copies(l, c)
            when(is_left, to_right.wait_send)
            when(is_right, to_left.wait_send)
            for cond, copy in forward_copies(l, c):
                when(cond, copy.wait_send)


def per_device(slabs, cols_count, rhs, dinv, spikes, merge_inv):
    _, _, orbs, width = rhs.shape
    half = dinv.shape[2]
    levels = spikes.shape[2]
    cw = min(64, width)
    chunks = width // cw
    bf16 = jnp.bfloat16
    vm = pltpu.VMEM
    dma = pltpu.SemaphoreType.DMA
    return pl.pallas_call(
        functools.partial(kernel, slabs, cols_count),
        out_shape=jax.ShapeDtypeStruct(rhs.shape, jnp.float32),
        in_specs=[pl.BlockSpec(memory_space=pltpu.VMEM)] + [pl.BlockSpec(memory_space=pltpu.HBM)] * 3,
        out_specs=pl.BlockSpec(memory_space=pltpu.VMEM),
        scratch_shapes=[
            vm((2, orbs, orbs), bf16),
            vm((2, levels, orbs, orbs), bf16),
            vm((2, orbs, orbs), bf16),
            vm((2, half // cols_count, orbs), bf16),
            vm((2, orbs, orbs), bf16),
            vm((2, orbs, orbs), bf16),
            vm((chunks, orbs, 2 * cw), bf16),
            vm((levels, chunks, orbs, 2 * cw), bf16),
            vm((chunks, orbs, 2 * cw), bf16),
            vm((orbs, 2 * cw), bf16),
            vm((orbs, 2 * cw), bf16),
            vm((levels, chunks, orbs, 2 * cw), bf16),
            vm((levels, chunks, orbs, 2 * cw), bf16),
            dma((2 + levels,)),
            dma((2 + levels,)),
            dma((2 + levels,)),
            dma((4,)),
            dma((4,)),
            dma((2, max(1, cols_count - 1))),
            dma((2, max(1, cols_count - 1))),
            dma((levels, chunks)),
            dma((levels, chunks)),
            dma((levels, chunks)),
        ],
        compiler_params=pltpu.CompilerParams(
            collective_id=0, has_side_effects=True, vmem_limit_bytes=56 * 1024 * 1024
        ),
    )(rhs, dinv, spikes, merge_inv)


def solution(mesh):
    placed = (
        P(None, ("energy", "slab"), None, ("col", "orb")),
        P(None, ("energy", "slab"), "orb", None),
        P(None, ("energy", "slab"), None, "orb", None),
        P(None, ("energy", "slab"), "orb", None),
    )
    return jax.shard_map(
        functools.partial(per_device, mesh.shape["slab"], mesh.shape["col"]),
        mesh=mesh,
        in_specs=placed,
        out_specs=P(None, ("energy", "slab"), None, ("col", "orb")),
        check_vma=False,
    )
```

```python
import functools

import jax
import jax.numpy as jnp
from jax import lax
from jax.experimental import pallas as pl
from jax.experimental.pallas import tpu as pltpu
from jax.sharding import PartitionSpec as P

MESH = pl.DeviceIdType.MESH


def kernel(
    slabs,
    cols_count,
    rhs_ref,
    dinv_ref,
    spikes_ref,
    merge_ref,
    out_ref,
    dfull,
    sfull,
    mfull,
    pown,
    pbuf,
    vbuf,
    xbuf,
    hbuf,
    ybuf,
    ibuf,
    tbuf,
    zbuf,
    tips,
    local_sem,
    orb_send,
    orb_recv,
    mat_send,
    mat_recv,
    share_send,
    share_recv,
    ex_send,
    fw_send,
    tip_recv,
):
    s = lax.axis_index("slab")
    o = lax.axis_index("orb")
    x = lax.axis_index("col")
    levels = sfull.shape[1]
    orbs = dfull.shape[1]
    half = dinv_ref.shape[2]
    chunks = xbuf.shape[0]
    cw = xbuf.shape[2] // 2
    rb = 256
    has_up = s < slabs - 1
    has_down = s > 0
    up = {"slab": s + 1}
    down = {"slab": s - 1}
    other = {"orb": 1 - o}
    mine = pl.ds(pl.multiple_of(o * half, half), half)
    piece = half // cols_count
    part = pl.ds(pl.multiple_of(x * piece, piece), piece)
    place = pl.ds(pl.multiple_of(o * half + x * piece, piece), piece)

    left_level = jnp.int32(0)
    right_level = jnp.int32(0)
    for l in range(levels):
        span = 1 << l
        pos = lax.rem(s, 2 * span)
        left_level = jnp.where(pos == span - 1, l, left_level)
        right_level = jnp.where(pos == span, l, right_level)

    def remote(src, dst, send, recv, to):
        return pltpu.make_async_remote_copy(
            src_ref=src, dst_ref=dst, send_sem=send, recv_sem=recv, device_id=to, device_id_type=MESH
        )

    def when(cond, fn):
        pl.when(cond)(fn)

    parts = [
        (spikes_ref.at[:, 0, left_level], sfull.at[:, left_level, mine]),
        (dinv_ref.at[:, 0], dfull.at[:, mine]),
        (merge_ref.at[:, 0], mfull.at[:, mine]),
    ]
    for k in range(1, levels):
        level = lax.rem(left_level + k, levels)
        parts.append((spikes_ref.at[:, 0, level], sfull.at[:, level, mine]))
    own = [pltpu.make_async_copy(a, b, local_sem.at[k]) for k, (a, b) in enumerate(parts)]
    for copy in own:
        copy.start()
    barrier = pltpu.get_barrier_semaphore()
    pl.semaphore_signal(barrier, inc=1, device_id=other, device_id_type=MESH)
    when(has_up, lambda: pl.semaphore_signal(barrier, inc=1, device_id=up, device_id_type=MESH))
    when(has_down, lambda: pl.semaphore_signal(barrier, inc=1, device_id=down, device_id_type=MESH))
    beside = [{"col": lax.rem(x + k, cols_count)} for k in range(1, cols_count)]
    for to in beside:
        pl.semaphore_signal(barrier, inc=1, device_id=to, device_id_type=MESH)
    pl.semaphore_wait(barrier, cols_count + jnp.where(has_up, 1, 0) + jnp.where(has_down, 1, 0))

    swaps = [remote(a, b, orb_send.at[k], orb_recv.at[k], other) for k, (a, b) in enumerate(parts)]
    for copy in swaps:
        copy.start()
    send_v = remote(spikes_ref.at[:, 0, right_level, part], vbuf.at[:, place], mat_send.at[0], mat_recv.at[0], down)
    send_p = remote(pown, pbuf.at[:, place], mat_send.at[1], mat_recv.at[1], up)
    share_v = [
        remote(vbuf.at[:, place], vbuf.at[:, place], share_send.at[0, k], share_recv.at[0, k], to)
        for k, to in enumerate(beside)
    ]
    share_p = [
        remote(pbuf.at[:, place], pbuf.at[:, place], share_send.at[1, k], share_recv.at[1, k], to)
        for k, to in enumerate(beside)
    ]
    pass_v = remote(vbuf.at[:, mine], vbuf.at[:, mine], mat_send.at[2], mat_recv.at[2], other)
    pass_p = remote(pbuf.at[:, mine], pbuf.at[:, mine], mat_send.at[3], mat_recv.at[3], other)
    when(has_down, send_v.start)

    def product(mat, x, emit):
        def body(r, carry):
            rows = pl.ds(pl.multiple_of(r * rb, rb), rb)
            a = jnp.dot(mat[0, rows, :], x[...], preferred_element_type=jnp.float32)
            b = jnp.dot(mat[1, rows, :], x[...], preferred_element_type=jnp.float32)
            emit(rows, a[:, :cw] - b[:, cw:], a[:, cw:] + b[:, :cw])
            return carry

        lax.fori_loop(0, orbs // rb, body, 0)

    own[0].wait()
    own[2].wait()
    swaps[0].wait_recv()

    @pl.when(has_up)
    def _():
        def body(j, carry):
            cols = pl.ds(pl.multiple_of(j * rb, rb), rb)
            re = sfull[0, left_level, :, cols]
            im = sfull[1, left_level, :, cols]
            m0 = mfull[0, place, :]
            m1 = mfull[1, place, :]
            dot = functools.partial(jnp.dot, preferred_element_type=jnp.float32)
            pown[0, :, cols] = (dot(m0, re) - dot(m1, im)).astype(jnp.bfloat16)
            pown[1, :, cols] = (dot(m0, im) + dot(m1, re)).astype(jnp.bfloat16)
            return carry

        lax.fori_loop(0, orbs // rb, body, 0)
        send_p.start()

    own[1].wait()
    swaps[1].wait_recv()
    swaps[2].wait_recv()

    def roles(l):
        span = 1 << l
        pos = lax.rem(s, 2 * span)
        return span, pos, pos == span - 1, pos == span

    def exchange_copies(l, c):
        send = ex_send.at[l, c]
        recv = tip_recv.at[l, c]
        return (
            remote(ybuf.at[c], tips.at[l, c], send, recv, up),
            remote(hbuf.at[l, c], tips.at[l, c], send, recv, down),
        )

    def forward_copies(l, c):
        span, pos, is_left, is_right = roles(l)
        send = fw_send.at[l, c]
        recv = tip_recv.at[l, c]
        out = []
        if span > 1:
            out = [
                (is_left, remote(zbuf.at[l, c], tips.at[l, c], send, recv, down)),
                (is_right, remote(zbuf.at[l, c], tips.at[l, c], send, recv, up)),
                ((pos > 0) & (pos < span - 1), remote(tips.at[l, c], tips.at[l, c], send, recv, down)),
                ((pos > span) & (pos < 2 * span - 1), remote(tips.at[l, c], tips.at[l, c], send, recv, up)),
            ]
        return out

    def offer(l, c):
        span, pos, is_left, is_right = roles(l)
        to_right, to_left = exchange_copies(l, c)

        @pl.when(is_right)
        def _():
            to_left.start()

        @pl.when(is_left)
        def _():
            def emit(rows, re, im):
                ybuf[c, rows, :cw] = re.astype(jnp.bfloat16)
                ybuf[c, rows, cw:] = im.astype(jnp.bfloat16)

            product(mfull, hbuf.at[l, c], emit)
            to_right.start()

    def settle(l, c):
        span, pos, is_left, is_right = roles(l)
        cols = pl.ds(c * cw, cw)
        spike = sfull.at[:, l]
        tip = tips.at[l, c]
        forwards = forward_copies(l, c)
        exchange_copies(l, c)[0].wait_recv()
        if span > 1:
            for cond, copy in forwards[2:]:
                when(cond, copy.start)

        @pl.when(is_right)
        def _():
            def emit(rows, re, im):
                zbuf[l, c, rows, :cw] = (tip[rows, :cw].astype(jnp.float32) - re).astype(jnp.bfloat16)
                zbuf[l, c, rows, cw:] = (tip[rows, cw:].astype(jnp.float32) - im).astype(jnp.bfloat16)

            product(pbuf, hbuf.at[l, c], emit)
            if span > 1:
                forwards[1][1].start()

        @pl.when(is_left)
        def _():
            def emit_interior(rows, re, im):
                ibuf[rows, :cw] = (out_ref[0, 0, rows, cols] - re).astype(jnp.bfloat16)
                ibuf[rows, cw:] = (out_ref[1, 0, rows, cols] - im).astype(jnp.bfloat16)

            def emit_left(rows, re, im):
                tbuf[rows, :cw] = re.astype(jnp.bfloat16)
                tbuf[rows, cw:] = im.astype(jnp.bfloat16)

            def emit_right(rows, re, im):
                zbuf[l, c, rows, :cw] = (tip[rows, :cw].astype(jnp.float32) - re).astype(jnp.bfloat16)
                zbuf[l, c, rows, cw:] = (tip[rows, cw:].astype(jnp.float32) - im).astype(jnp.bfloat16)

            product(spike, tip, emit_interior)
            product(mfull, ibuf, emit_left)
            product(vbuf, tbuf, emit_right)
            if span > 1:
                forwards[0][1].start()

        def update(z):
            def emit(rows, re, im):
                re = out_ref[0, 0, rows, cols] - re
                im = out_ref[1, 0, rows, cols] - im
                out_ref[0, 0, rows, cols] = re
                out_ref[1, 0, rows, cols] = im
                if l + 1 < levels:
                    hbuf[l + 1, c, rows, :cw] = re.astype(jnp.bfloat16)
                    hbuf[l + 1, c, rows, cw:] = im.astype(jnp.bfloat16)

            product(spike, z, emit)

        if span == 1:
            update(zbuf.at[l, c])
        else:
            interface = is_left | is_right
            when(interface, lambda: update(zbuf.at[l, c]))
            when(jnp.logical_not(interface), lambda: update(tip))

    for c in range(chunks):
        cols = pl.ds(c * cw, cw)
        xbuf[c, :, :cw] = rhs_ref[0, 0, :, cols]
        xbuf[c, :, cw:] = rhs_ref[1, 0, :, cols]

        def emit(rows, re, im, c=c, cols=cols):
            out_ref[0, 0, rows, cols] = re
            out_ref[1, 0, rows, cols] = im
            hbuf[0, c, rows, :cw] = re.astype(jnp.bfloat16)
            hbuf[0, c, rows, cw:] = im.astype(jnp.bfloat16)

        product(dfull, xbuf.at[c], emit)
        offer(0, c)

    def run(copies, name):
        def go():
            for copy in copies:
                getattr(copy, name)()

        return go

    for k in range(3, len(parts)):
        own[k].wait()
        swaps[k].wait_recv()

    @pl.when(has_up)
    def _():
        send_v.wait_recv()
        run(share_v, "start")()

    @pl.when(has_down)
    def _():
        send_p.wait_recv()
        run(share_p, "start")()

    @pl.when(has_up)
    def _():
        run(share_v, "wait_recv")()
        pass_v.start()

    @pl.when(has_down)
    def _():
        run(share_p, "wait_recv")()
        pass_p.start()

    when(has_up, pass_v.wait_recv)
    when(has_down, pass_p.wait_recv)

    for l in range(levels):
        for c in range(chunks):
            settle(l, c)
            if l + 1 < levels:
                offer(l + 1, c)

    for copy in swaps:
        copy.wait_send()
    when(has_down, send_v.wait_send)
    when(has_up, send_p.wait_send)
    when(has_up, run(share_v, "wait_send"))
    when(has_down, run(share_p, "wait_send"))
    when(has_up, pass_v.wait_send)
    when(has_down, pass_p.wait_send)
    for l in range(levels):
        span, pos, is_left, is_right = roles(l)
        for c in range(chunks):
            to_right, to_left = exchange_copies(l, c)
            when(is_left, to_right.wait_send)
            when(is_right, to_left.wait_send)
            for cond, copy in forward_copies(l, c):
                when(cond, copy.wait_send)


def per_device(slabs, cols_count, rhs, dinv, spikes, merge_inv):
    _, _, orbs, width = rhs.shape
    half = dinv.shape[2]
    levels = spikes.shape[2]
    cw = min(128, width)
    chunks = width // cw
    bf16 = jnp.bfloat16
    vm = pltpu.VMEM
    dma = pltpu.SemaphoreType.DMA
    return pl.pallas_call(
        functools.partial(kernel, slabs, cols_count),
        out_shape=jax.ShapeDtypeStruct(rhs.shape, jnp.float32),
        in_specs=[pl.BlockSpec(memory_space=pltpu.VMEM)] + [pl.BlockSpec(memory_space=pltpu.HBM)] * 3,
        out_specs=pl.BlockSpec(memory_space=pltpu.VMEM),
        scratch_shapes=[
            vm((2, orbs, orbs), bf16),
            vm((2, levels, orbs, orbs), bf16),
            vm((2, orbs, orbs), bf16),
            vm((2, half // cols_count, orbs), bf16),
            vm((2, orbs, orbs), bf16),
            vm((2, orbs, orbs), bf16),
            vm((chunks, orbs, 2 * cw), bf16),
            vm((levels, chunks, orbs, 2 * cw), bf16),
            vm((chunks, orbs, 2 * cw), bf16),
            vm((orbs, 2 * cw), bf16),
            vm((orbs, 2 * cw), bf16),
            vm((levels, chunks, orbs, 2 * cw), bf16),
            vm((levels, chunks, orbs, 2 * cw), bf16),
            dma((2 + levels,)),
            dma((2 + levels,)),
            dma((2 + levels,)),
            dma((4,)),
            dma((4,)),
            dma((2, max(1, cols_count - 1))),
            dma((2, max(1, cols_count - 1))),
            dma((levels, chunks)),
            dma((levels, chunks)),
            dma((levels, chunks)),
        ],
        compiler_params=pltpu.CompilerParams(
            collective_id=0, has_side_effects=True, vmem_limit_bytes=56 * 1024 * 1024
        ),
    )(rhs, dinv, spikes, merge_inv)


def solution(mesh):
    placed = (
        P(None, ("energy", "slab"), None, ("col", "orb")),
        P(None, ("energy", "slab"), "orb", None),
        P(None, ("energy", "slab"), None, "orb", None),
        P(None, ("energy", "slab"), "orb", None),
    )
    return jax.shard_map(
        functools.partial(per_device, mesh.shape["slab"], mesh.shape["col"]),
        mesh=mesh,
        in_specs=placed,
        out_specs=P(None, ("energy", "slab"), None, ("col", "orb")),
        check_vma=False,
    )
```

```python
import functools

import jax
import jax.numpy as jnp
from jax import lax
from jax.experimental import pallas as pl
from jax.experimental.pallas import tpu as pltpu
from jax.sharding import PartitionSpec as P

MESH = pl.DeviceIdType.MESH


def kernel(
    slabs,
    cols_count,
    rhs_ref,
    dinv_ref,
    spikes_ref,
    merge_ref,
    out_ref,
    dfull,
    sfull,
    mfull,
    pown,
    pbuf,
    vbuf,
    xbuf,
    hbuf,
    ybuf,
    ibuf,
    tbuf,
    zbuf,
    tips,
    local_sem,
    orb_send,
    orb_recv,
    mat_send,
    mat_recv,
    share_send,
    share_recv,
    ex_send,
    fw_send,
    tip_recv,
):
    s = lax.axis_index("slab")
    o = lax.axis_index("orb")
    x = lax.axis_index("col")
    levels = sfull.shape[1]
    orbs = dfull.shape[1]
    half = dinv_ref.shape[2]
    chunks = xbuf.shape[0]
    cw = xbuf.shape[2] // 2
    rb = 256
    tall = orbs
    has_up = s < slabs - 1
    has_down = s > 0
    up = {"slab": s + 1}
    down = {"slab": s - 1}
    other = {"orb": 1 - o}
    mine = pl.ds(pl.multiple_of(o * half, half), half)
    piece = half // cols_count
    part = pl.ds(pl.multiple_of(x * piece, piece), piece)
    place = pl.ds(pl.multiple_of(o * half + x * piece, piece), piece)

    left_level = jnp.int32(0)
    right_level = jnp.int32(0)
    for l in range(levels):
        span = 1 << l
        pos = lax.rem(s, 2 * span)
        left_level = jnp.where(pos == span - 1, l, left_level)
        right_level = jnp.where(pos == span, l, right_level)

    def remote(src, dst, send, recv, to):
        return pltpu.make_async_remote_copy(
            src_ref=src, dst_ref=dst, send_sem=send, recv_sem=recv, device_id=to, device_id_type=MESH
        )

    def when(cond, fn):
        pl.when(cond)(fn)

    parts = [
        (dinv_ref.at[:, 0], dfull.at[:, mine]),
        (spikes_ref.at[:, 0, left_level], sfull.at[:, left_level, mine]),
        (merge_ref.at[:, 0], mfull.at[:, mine]),
    ]
    for k in range(1, levels):
        level = lax.rem(left_level + k, levels)
        parts.append((spikes_ref.at[:, 0, level], sfull.at[:, level, mine]))
    own = [pltpu.make_async_copy(a, b, local_sem.at[k]) for k, (a, b) in enumerate(parts)]
    for copy in own:
        copy.start()
    barrier = pltpu.get_barrier_semaphore()
    pl.semaphore_signal(barrier, inc=1, device_id=other, device_id_type=MESH)
    when(has_up, lambda: pl.semaphore_signal(barrier, inc=1, device_id=up, device_id_type=MESH))
    when(has_down, lambda: pl.semaphore_signal(barrier, inc=1, device_id=down, device_id_type=MESH))
    beside = [{"col": lax.rem(x + k, cols_count)} for k in range(1, cols_count)]
    for to in beside:
        pl.semaphore_signal(barrier, inc=1, device_id=to, device_id_type=MESH)
    pl.semaphore_wait(barrier, cols_count + jnp.where(has_up, 1, 0) + jnp.where(has_down, 1, 0))

    swaps = [remote(a, b, orb_send.at[k], orb_recv.at[k], other) for k, (a, b) in enumerate(parts)]
    for copy in swaps:
        copy.start()
    send_v = remote(spikes_ref.at[:, 0, right_level, part], vbuf.at[:, place], mat_send.at[0], mat_recv.at[0], down)
    send_p = remote(pown, pbuf.at[:, place], mat_send.at[1], mat_recv.at[1], up)
    share_v = [
        remote(vbuf.at[:, place], vbuf.at[:, place], share_send.at[0, k], share_recv.at[0, k], to)
        for k, to in enumerate(beside)
    ]
    share_p = [
        remote(pbuf.at[:, place], pbuf.at[:, place], share_send.at[1, k], share_recv.at[1, k], to)
        for k, to in enumerate(beside)
    ]
    pass_v = remote(vbuf.at[:, mine], vbuf.at[:, mine], mat_send.at[2], mat_recv.at[2], other)
    pass_p = remote(pbuf.at[:, mine], pbuf.at[:, mine], mat_send.at[3], mat_recv.at[3], other)
    when(has_down, send_v.start)

    def product(mat, x, emit):
        def body(r, carry):
            rows = pl.ds(pl.multiple_of(r * tall, tall), tall)
            a = jnp.dot(mat[0, rows, :], x[...], preferred_element_type=jnp.float32)
            b = jnp.dot(mat[1, rows, :], x[...], preferred_element_type=jnp.float32)
            emit(rows, a[:, :cw] - b[:, cw:], a[:, cw:] + b[:, :cw])
            return carry

        lax.fori_loop(0, orbs // tall, body, 0)

    p_out = has_up & (left_level > 0)
    p_in = has_down & (right_level > 0)
    own[0].wait()
    swaps[0].wait_recv()

    def roles(l):
        span = 1 << l
        pos = lax.rem(s, 2 * span)
        return span, pos, pos == span - 1, pos == span

    def exchange_copies(l, c):
        send = ex_send.at[l, c]
        recv = tip_recv.at[l, c]
        return (
            remote(ybuf.at[c], tips.at[l, c], send, recv, up),
            remote(hbuf.at[l, c], tips.at[l, c], send, recv, down),
        )

    def forward_copies(l, c):
        span, pos, is_left, is_right = roles(l)
        send = fw_send.at[l, c]
        recv = tip_recv.at[l, c]
        out = []
        if span > 1:
            out = [
                (is_left, remote(zbuf.at[l, c], tips.at[l, c], send, recv, down)),
                (is_right, remote(zbuf.at[l, c], tips.at[l, c], send, recv, up)),
                ((pos > 0) & (pos < span - 1), remote(tips.at[l, c], tips.at[l, c], send, recv, down)),
                ((pos > span) & (pos < 2 * span - 1), remote(tips.at[l, c], tips.at[l, c], send, recv, up)),
            ]
        return out

    def offer(l, c):
        span, pos, is_left, is_right = roles(l)
        to_right, to_left = exchange_copies(l, c)

        @pl.when(is_right)
        def _():
            to_left.start()

        if l == 0:
            return

        @pl.when(is_left)
        def _():
            def emit(rows, re, im):
                ybuf[c, rows, :cw] = re.astype(jnp.bfloat16)
                ybuf[c, rows, cw:] = im.astype(jnp.bfloat16)

            product(mfull, hbuf.at[l, c], emit)
            to_right.start()

    def emit_to(ref):
        def emit(rows, re, im):
            ref[rows, :cw] = re.astype(jnp.bfloat16)
            ref[rows, cw:] = im.astype(jnp.bfloat16)

        return emit

    def tip_of_left(c):
        cols = pl.ds(c * cw, cw)

        @pl.when(roles(0)[2])
        def _():
            to_right, to_left = exchange_copies(0, c)
            to_left.wait_recv()

            def emit_interior(rows, re, im):
                ibuf[rows, :cw] = (out_ref[0, 0, rows, cols] - re).astype(jnp.bfloat16)
                ibuf[rows, cw:] = (out_ref[1, 0, rows, cols] - im).astype(jnp.bfloat16)

            product(sfull.at[:, 0], tips.at[0, c], emit_interior)
            product(mfull, ibuf, emit_to(ybuf.at[c]))
            to_right.start()

    def settle(l, c):
        span, pos, is_left, is_right = roles(l)
        cols = pl.ds(c * cw, cw)
        spike = sfull.at[:, l]
        tip = tips.at[l, c]
        forwards = forward_copies(l, c)
        if span > 1:
            exchange_copies(l, c)[0].wait_recv()
        else:
            when(is_right, exchange_copies(l, c)[0].wait_recv)
        if span > 1:
            for cond, copy in forwards[2:]:
                when(cond, copy.start)

        @pl.when(is_right & (span > 1))
        def _():
            def emit(rows, re, im):
                zbuf[l, c, rows, :cw] = (tip[rows, :cw].astype(jnp.float32) - re).astype(jnp.bfloat16)
                zbuf[l, c, rows, cw:] = (tip[rows, cw:].astype(jnp.float32) - im).astype(jnp.bfloat16)

            if span > 1:
                product(pbuf, hbuf.at[l, c], emit)
            if span > 1:
                forwards[1][1].start()

        @pl.when(is_left)
        def _():
            def emit_interior(rows, re, im):
                ibuf[rows, :cw] = (out_ref[0, 0, rows, cols] - re).astype(jnp.bfloat16)
                ibuf[rows, cw:] = (out_ref[1, 0, rows, cols] - im).astype(jnp.bfloat16)

            def emit_left(rows, re, im):
                tbuf[rows, :cw] = re.astype(jnp.bfloat16)
                tbuf[rows, cw:] = im.astype(jnp.bfloat16)

            def emit_right(rows, re, im):
                zbuf[l, c, rows, :cw] = (tip[rows, :cw].astype(jnp.float32) - re).astype(jnp.bfloat16)
                zbuf[l, c, rows, cw:] = (tip[rows, cw:].astype(jnp.float32) - im).astype(jnp.bfloat16)

            if span > 1:
                product(spike, tip, emit_interior)
                product(mfull, ibuf, emit_left)
                product(vbuf, tbuf, emit_right)
            else:
                product(vbuf, ybuf.at[c], emit_right)
            if span > 1:
                forwards[0][1].start()

        def update(z):
            def emit(rows, re, im):
                re = out_ref[0, 0, rows, cols] - re
                im = out_ref[1, 0, rows, cols] - im
                out_ref[0, 0, rows, cols] = re
                out_ref[1, 0, rows, cols] = im
                if l + 1 < levels:
                    hbuf[l + 1, c, rows, :cw] = re.astype(jnp.bfloat16)
                    hbuf[l + 1, c, rows, cw:] = im.astype(jnp.bfloat16)

            product(spike, z, emit)

        if span == 1:
            when(is_left, lambda: update(zbuf.at[l, c]))
            when(is_right, lambda: update(tip))
        else:
            interface = is_left | is_right
            when(interface, lambda: update(zbuf.at[l, c]))
            when(jnp.logical_not(interface), lambda: update(tip))

    for c in range(chunks):
        cols = pl.ds(c * cw, cw)
        xbuf[c, :, :cw] = rhs_ref[0, 0, :, cols]
        xbuf[c, :, cw:] = rhs_ref[1, 0, :, cols]

        def emit(rows, re, im, c=c, cols=cols):
            out_ref[0, 0, rows, cols] = re
            out_ref[1, 0, rows, cols] = im
            hbuf[0, c, rows, :cw] = re.astype(jnp.bfloat16)
            hbuf[0, c, rows, cw:] = im.astype(jnp.bfloat16)

        product(dfull, xbuf.at[c], emit)
        offer(0, c)

    def run(copies, name):
        def go():
            for copy in copies:
                getattr(copy, name)()

        return go

    for k in range(1, len(parts)):
        own[k].wait()
        swaps[k].wait_recv()

    @pl.when(p_out)
    def _():
        def body(j, carry):
            cols = pl.ds(pl.multiple_of(j * rb, rb), rb)
            re = sfull[0, left_level, :, cols]
            im = sfull[1, left_level, :, cols]
            m0 = mfull[0, place, :]
            m1 = mfull[1, place, :]
            dot = functools.partial(jnp.dot, preferred_element_type=jnp.float32)
            pown[0, :, cols] = (dot(m0, re) - dot(m1, im)).astype(jnp.bfloat16)
            pown[1, :, cols] = (dot(m0, im) + dot(m1, re)).astype(jnp.bfloat16)
            return carry

        lax.fori_loop(0, orbs // rb, body, 0)
        send_p.start()

    @pl.when(has_up)
    def _():
        send_v.wait_recv()
        run(share_v, "start")()

    for c in range(chunks):
        tip_of_left(c)
        if c == chunks // 2 - 1 or chunks == 1:

            @pl.when(has_up)
            def _():
                run(share_v, "wait_recv")()
                pass_v.start()

        if c == max(0, chunks - 2):

            @pl.when(p_in)
            def _():
                send_p.wait_recv()
                run(share_p, "start")()

    when(has_up, pass_v.wait_recv)

    for l in range(levels):
        if l == 1:

            @pl.when(p_in)
            def _():
                run(share_p, "wait_recv")()
                pass_p.start()
                pass_p.wait_recv()

        for c in range(chunks):
            settle(l, c)
            if l + 1 < levels:
                offer(l + 1, c)

    for copy in swaps:
        copy.wait_send()
    when(has_down, send_v.wait_send)
    when(p_out, send_p.wait_send)
    when(has_up, run(share_v, "wait_send"))
    when(p_in, run(share_p, "wait_send"))
    when(has_up, pass_v.wait_send)
    when(p_in, pass_p.wait_send)
    for l in range(levels):
        span, pos, is_left, is_right = roles(l)
        for c in range(chunks):
            to_right, to_left = exchange_copies(l, c)
            when(is_left, to_right.wait_send)
            when(is_right, to_left.wait_send)
            for cond, copy in forward_copies(l, c):
                when(cond, copy.wait_send)


def per_device(slabs, cols_count, rhs, dinv, spikes, merge_inv):
    _, _, orbs, width = rhs.shape
    half = dinv.shape[2]
    levels = spikes.shape[2]
    cw = min(64, width)
    chunks = width // cw
    bf16 = jnp.bfloat16
    vm = pltpu.VMEM
    dma = pltpu.SemaphoreType.DMA
    return pl.pallas_call(
        functools.partial(kernel, slabs, cols_count),
        out_shape=jax.ShapeDtypeStruct(rhs.shape, jnp.float32),
        in_specs=[pl.BlockSpec(memory_space=pltpu.VMEM)] + [pl.BlockSpec(memory_space=pltpu.HBM)] * 3,
        out_specs=pl.BlockSpec(memory_space=pltpu.VMEM),
        scratch_shapes=[
            vm((2, orbs, orbs), bf16),
            vm((2, levels, orbs, orbs), bf16),
            vm((2, orbs, orbs), bf16),
            vm((2, half // cols_count, orbs), bf16),
            vm((2, orbs, orbs), bf16),
            vm((2, orbs, orbs), bf16),
            vm((chunks, orbs, 2 * cw), bf16),
            vm((levels, chunks, orbs, 2 * cw), bf16),
            vm((chunks, orbs, 2 * cw), bf16),
            vm((orbs, 2 * cw), bf16),
            vm((orbs, 2 * cw), bf16),
            vm((levels, chunks, orbs, 2 * cw), bf16),
            vm((levels, chunks, orbs, 2 * cw), bf16),
            dma((2 + levels,)),
            dma((2 + levels,)),
            dma((2 + levels,)),
            dma((4,)),
            dma((4,)),
            dma((2, max(1, cols_count - 1))),
            dma((2, max(1, cols_count - 1))),
            dma((levels, chunks)),
            dma((levels, chunks)),
            dma((levels, chunks)),
        ],
        compiler_params=pltpu.CompilerParams(
            collective_id=0, has_side_effects=True, vmem_limit_bytes=56 * 1024 * 1024
        ),
    )(rhs, dinv, spikes, merge_inv)


def solution(mesh):
    placed = (
        P(None, ("energy", "slab"), None, ("col", "orb")),
        P(None, ("energy", "slab"), "orb", None),
        P(None, ("energy", "slab"), None, "orb", None),
        P(None, ("energy", "slab"), "orb", None),
    )
    return jax.shard_map(
        functools.partial(per_device, mesh.shape["slab"], mesh.shape["col"]),
        mesh=mesh,
        in_specs=placed,
        out_specs=P(None, ("energy", "slab"), None, ("col", "orb")),
        check_vma=False,
    )
```

```python
import functools

import jax
import jax.numpy as jnp
from jax import lax
from jax.experimental import pallas as pl
from jax.experimental.pallas import tpu as pltpu
from jax.sharding import PartitionSpec as P

MESH = pl.DeviceIdType.MESH


def kernel(
    slabs,
    cols_count,
    rhs_ref,
    dinv_ref,
    spikes_ref,
    merge_ref,
    out_ref,
    dfull,
    sfull,
    mfull,
    pown,
    pbuf,
    vbuf,
    xbuf,
    hbuf,
    ybuf,
    ibuf,
    tbuf,
    zbuf,
    tips,
    local_sem,
    orb_send,
    orb_recv,
    mat_send,
    mat_recv,
    share_send,
    share_recv,
    ex_send,
    fw_send,
    tip_recv,
):
    s = lax.axis_index("slab")
    o = lax.axis_index("orb")
    x = lax.axis_index("col")
    levels = sfull.shape[1]
    orbs = dfull.shape[1]
    half = dinv_ref.shape[2]
    chunks = xbuf.shape[0]
    cw = xbuf.shape[2] // 2
    rb = 256
    tall = orbs
    has_up = s < slabs - 1
    has_down = s > 0
    up = {"slab": s + 1}
    down = {"slab": s - 1}
    other = {"orb": 1 - o}
    mine = pl.ds(pl.multiple_of(o * half, half), half)
    piece = half // cols_count
    part = pl.ds(pl.multiple_of(x * piece, piece), piece)
    place = pl.ds(pl.multiple_of(o * half + x * piece, piece), piece)

    left_level = jnp.int32(0)
    right_level = jnp.int32(0)
    for l in range(levels):
        span = 1 << l
        pos = lax.rem(s, 2 * span)
        left_level = jnp.where(pos == span - 1, l, left_level)
        right_level = jnp.where(pos == span, l, right_level)

    def remote(src, dst, send, recv, to):
        return pltpu.make_async_remote_copy(
            src_ref=src, dst_ref=dst, send_sem=send, recv_sem=recv, device_id=to, device_id_type=MESH
        )

    def when(cond, fn):
        pl.when(cond)(fn)

    parts = [
        (dinv_ref.at[:, 0], dfull.at[:, mine]),
        (spikes_ref.at[:, 0, left_level], sfull.at[:, left_level, mine]),
        (merge_ref.at[:, 0], mfull.at[:, mine]),
    ]
    for k in range(1, levels):
        level = lax.rem(left_level + k, levels)
        parts.append((spikes_ref.at[:, 0, level], sfull.at[:, level, mine]))
    own = [pltpu.make_async_copy(a, b, local_sem.at[k]) for k, (a, b) in enumerate(parts)]
    for copy in own:
        copy.start()
    barrier = pltpu.get_barrier_semaphore()
    pl.semaphore_signal(barrier, inc=1, device_id=other, device_id_type=MESH)
    when(has_up, lambda: pl.semaphore_signal(barrier, inc=1, device_id=up, device_id_type=MESH))
    when(has_down, lambda: pl.semaphore_signal(barrier, inc=1, device_id=down, device_id_type=MESH))
    beside = [{"col": lax.rem(x + k, cols_count)} for k in range(1, cols_count)]
    for to in beside:
        pl.semaphore_signal(barrier, inc=1, device_id=to, device_id_type=MESH)
    pl.semaphore_wait(barrier, cols_count + jnp.where(has_up, 1, 0) + jnp.where(has_down, 1, 0))

    swaps = [remote(a, b, orb_send.at[k], orb_recv.at[k], other) for k, (a, b) in enumerate(parts)]
    for copy in swaps:
        copy.start()
    send_v = remote(spikes_ref.at[:, 0, right_level, part], vbuf.at[:, place], mat_send.at[0], mat_recv.at[0], down)
    send_p = remote(pown, pbuf.at[:, place], mat_send.at[1], mat_recv.at[1], up)
    share_v = [
        remote(vbuf.at[:, place], vbuf.at[:, place], share_send.at[0, k], share_recv.at[0, k], to)
        for k, to in enumerate(beside)
    ]
    share_p = [
        remote(pbuf.at[:, place], pbuf.at[:, place], share_send.at[1, k], share_recv.at[1, k], to)
        for k, to in enumerate(beside)
    ]
    pass_v = remote(vbuf.at[:, mine], vbuf.at[:, mine], mat_send.at[2], mat_recv.at[2], other)
    pass_p = remote(pbuf.at[:, mine], pbuf.at[:, mine], mat_send.at[3], mat_recv.at[3], other)
    when(has_down, send_v.start)

    def product(mat, x, emit):
        def body(r, carry):
            rows = pl.ds(pl.multiple_of(r * tall, tall), tall)
            a = jnp.dot(mat[0, rows, :], x[...], preferred_element_type=jnp.float32)
            b = jnp.dot(mat[1, rows, :], x[...], preferred_element_type=jnp.float32)
            emit(rows, a[:, :cw] - b[:, cw:], a[:, cw:] + b[:, :cw])
            return carry

        lax.fori_loop(0, orbs // tall, body, 0)

    p_out = has_up & (left_level > 0)
    p_in = has_down & (right_level > 0)
    own[0].wait()
    swaps[0].wait_recv()

    def roles(l):
        span = 1 << l
        pos = lax.rem(s, 2 * span)
        return span, pos, pos == span - 1, pos == span

    def exchange_copies(l, c):
        send = ex_send.at[l, c]
        recv = tip_recv.at[l, c]
        return (
            remote(ybuf.at[c], tips.at[l, c], send, recv, up),
            remote(hbuf.at[l, c], tips.at[l, c], send, recv, down),
        )

    def forward_copies(l, c):
        span, pos, is_left, is_right = roles(l)
        send = fw_send.at[l, c]
        recv = tip_recv.at[l, c]
        out = []
        if span > 1:
            out = [
                (is_left, remote(zbuf.at[l, c], tips.at[l, c], send, recv, down)),
                (is_right, remote(zbuf.at[l, c], tips.at[l, c], send, recv, up)),
                ((pos > 0) & (pos < span - 1), remote(tips.at[l, c], tips.at[l, c], send, recv, down)),
                ((pos > span) & (pos < 2 * span - 1), remote(tips.at[l, c], tips.at[l, c], send, recv, up)),
            ]
        return out

    def offer(l, c):
        span, pos, is_left, is_right = roles(l)
        to_right, to_left = exchange_copies(l, c)

        @pl.when(is_right)
        def _():
            to_left.start()

        if l == 0:
            return

        @pl.when(is_left)
        def _():
            def emit(rows, re, im):
                ybuf[c, rows, :cw] = re.astype(jnp.bfloat16)
                ybuf[c, rows, cw:] = im.astype(jnp.bfloat16)

            product(mfull, hbuf.at[l, c], emit)
            to_right.start()

    def emit_to(ref):
        def emit(rows, re, im):
            ref[rows, :cw] = re.astype(jnp.bfloat16)
            ref[rows, cw:] = im.astype(jnp.bfloat16)

        return emit

    def tip_of_left(c):
        cols = pl.ds(c * cw, cw)

        @pl.when(roles(0)[2])
        def _():
            to_right, to_left = exchange_copies(0, c)
            to_left.wait_recv()

            def emit_interior(rows, re, im):
                ibuf[rows, :cw] = (out_ref[0, 0, rows, cols] - re).astype(jnp.bfloat16)
                ibuf[rows, cw:] = (out_ref[1, 0, rows, cols] - im).astype(jnp.bfloat16)

            product(sfull.at[:, 0], tips.at[0, c], emit_interior)
            product(mfull, ibuf, emit_to(ybuf.at[c]))
            to_right.start()

    def settle(l, c):
        span, pos, is_left, is_right = roles(l)
        cols = pl.ds(c * cw, cw)
        spike = sfull.at[:, l]
        tip = tips.at[l, c]
        forwards = forward_copies(l, c)
        if span > 1:
            exchange_copies(l, c)[0].wait_recv()
        else:
            when(is_right, exchange_copies(l, c)[0].wait_recv)
        if span > 1:
            for cond, copy in forwards[2:]:
                when(cond, copy.start)

        @pl.when(is_right & (span > 1))
        def _():
            def emit(rows, re, im):
                zbuf[l, c, rows, :cw] = (tip[rows, :cw].astype(jnp.float32) - re).astype(jnp.bfloat16)
                zbuf[l, c, rows, cw:] = (tip[rows, cw:].astype(jnp.float32) - im).astype(jnp.bfloat16)

            if span > 1:
                product(pbuf, hbuf.at[l, c], emit)
            if span > 1:
                forwards[1][1].start()

        @pl.when(is_left)
        def _():
            def emit_interior(rows, re, im):
                ibuf[rows, :cw] = (out_ref[0, 0, rows, cols] - re).astype(jnp.bfloat16)
                ibuf[rows, cw:] = (out_ref[1, 0, rows, cols] - im).astype(jnp.bfloat16)

            def emit_left(rows, re, im):
                tbuf[rows, :cw] = re.astype(jnp.bfloat16)
                tbuf[rows, cw:] = im.astype(jnp.bfloat16)

            def emit_right(rows, re, im):
                zbuf[l, c, rows, :cw] = (tip[rows, :cw].astype(jnp.float32) - re).astype(jnp.bfloat16)
                zbuf[l, c, rows, cw:] = (tip[rows, cw:].astype(jnp.float32) - im).astype(jnp.bfloat16)

            if span > 1:
                product(spike, tip, emit_interior)
                product(mfull, ibuf, emit_left)
                product(vbuf, tbuf, emit_right)
            else:
                product(vbuf, ybuf.at[c], emit_right)
            if span > 1:
                forwards[0][1].start()

        def update(z):
            def emit(rows, re, im):
                re = out_ref[0, 0, rows, cols] - re
                im = out_ref[1, 0, rows, cols] - im
                out_ref[0, 0, rows, cols] = re
                out_ref[1, 0, rows, cols] = im
                if l + 1 < levels:
                    hbuf[l + 1, c, rows, :cw] = re.astype(jnp.bfloat16)
                    hbuf[l + 1, c, rows, cw:] = im.astype(jnp.bfloat16)

            product(spike, z, emit)

        if span == 1:
            when(is_left, lambda: update(zbuf.at[l, c]))
            when(is_right, lambda: update(tip))
        else:
            interface = is_left | is_right
            when(interface, lambda: update(zbuf.at[l, c]))
            when(jnp.logical_not(interface), lambda: update(tip))

    for c in range(chunks):
        cols = pl.ds(c * cw, cw)
        xbuf[c, :, :cw] = rhs_ref[0, 0, :, cols]
        xbuf[c, :, cw:] = rhs_ref[1, 0, :, cols]

        def emit(rows, re, im, c=c, cols=cols):
            out_ref[0, 0, rows, cols] = re
            out_ref[1, 0, rows, cols] = im
            hbuf[0, c, rows, :cw] = re.astype(jnp.bfloat16)
            hbuf[0, c, rows, cw:] = im.astype(jnp.bfloat16)

        product(dfull, xbuf.at[c], emit)
        offer(0, c)

    def run(copies, name):
        def go():
            for copy in copies:
                getattr(copy, name)()

        return go

    for k in range(1, len(parts)):
        own[k].wait()
        swaps[k].wait_recv()

    @pl.when(p_out)
    def _():
        def body(j, carry):
            cols = pl.ds(pl.multiple_of(j * rb, rb), rb)
            re = sfull[0, left_level, :, cols]
            im = sfull[1, left_level, :, cols]
            m0 = mfull[0, place, :]
            m1 = mfull[1, place, :]
            dot = functools.partial(jnp.dot, preferred_element_type=jnp.float32)
            pown[0, :, cols] = (dot(m0, re) - dot(m1, im)).astype(jnp.bfloat16)
            pown[1, :, cols] = (dot(m0, im) + dot(m1, re)).astype(jnp.bfloat16)
            return carry

        lax.fori_loop(0, orbs // rb, body, 0)
        send_p.start()

    @pl.when(has_up)
    def _():
        send_v.wait_recv()
        run(share_v, "start")()

    for c in range(chunks):
        tip_of_left(c)
        if c == chunks // 2 - 1 or chunks == 1:

            @pl.when(has_up)
            def _():
                run(share_v, "wait_recv")()
                pass_v.start()

        if c == max(0, chunks - 2):

            @pl.when(p_in)
            def _():
                send_p.wait_recv()
                run(share_p, "start")()

    when(has_up, pass_v.wait_recv)

    for l in range(levels):
        if l == 1:

            @pl.when(p_in)
            def _():
                run(share_p, "wait_recv")()
                pass_p.start()
                pass_p.wait_recv()

        for c in range(chunks):
            settle(l, c)
            if l + 1 < levels:
                offer(l + 1, c)

    for copy in swaps:
        copy.wait_send()
    when(has_down, send_v.wait_send)
    when(p_out, send_p.wait_send)
    when(has_up, run(share_v, "wait_send"))
    when(p_in, run(share_p, "wait_send"))
    when(has_up, pass_v.wait_send)
    when(p_in, pass_p.wait_send)
    for l in range(levels):
        span, pos, is_left, is_right = roles(l)
        for c in range(chunks):
            to_right, to_left = exchange_copies(l, c)
            when(is_left, to_right.wait_send)
            when(is_right, to_left.wait_send)
            for cond, copy in forward_copies(l, c):
                when(cond, copy.wait_send)


def per_device(slabs, cols_count, rhs, dinv, spikes, merge_inv):
    _, _, orbs, width = rhs.shape
    half = dinv.shape[2]
    levels = spikes.shape[2]
    cw = min(64, width)
    chunks = width // cw
    bf16 = jnp.bfloat16
    vm = pltpu.VMEM
    dma = pltpu.SemaphoreType.DMA
    return pl.pallas_call(
        functools.partial(kernel, slabs, cols_count),
        out_shape=jax.ShapeDtypeStruct(rhs.shape, jnp.float32),
        in_specs=[pl.BlockSpec(memory_space=pltpu.VMEM)] + [pl.BlockSpec(memory_space=pltpu.HBM)] * 3,
        out_specs=pl.BlockSpec(memory_space=pltpu.VMEM),
        scratch_shapes=[
            vm((2, orbs, orbs), bf16),
            vm((2, levels, orbs, orbs), bf16),
            vm((2, orbs, orbs), bf16),
            vm((2, half // cols_count, orbs), bf16),
            vm((2, orbs, orbs), bf16),
            vm((2, orbs, orbs), bf16),
            vm((chunks, orbs, 2 * cw), bf16),
            vm((levels, chunks, orbs, 2 * cw), bf16),
            vm((chunks, orbs, 2 * cw), bf16),
            vm((orbs, 2 * cw), bf16),
            vm((orbs, 2 * cw), bf16),
            vm((levels, chunks, orbs, 2 * cw), bf16),
            vm((levels, chunks, orbs, 2 * cw), bf16),
            dma((2 + levels,)),
            dma((2 + levels,)),
            dma((2 + levels,)),
            dma((4,)),
            dma((4,)),
            dma((2, max(1, cols_count - 1))),
            dma((2, max(1, cols_count - 1))),
            dma((levels, chunks)),
            dma((levels, chunks)),
            dma((levels, chunks)),
        ],
        compiler_params=pltpu.CompilerParams(
            collective_id=0, has_side_effects=True, vmem_limit_bytes=24 * 1024 * 1024
        ),
    )(rhs, *(pltpu.with_memory_space_constraint(m, pltpu.HBM) for m in (dinv, spikes, merge_inv)))


def solution(mesh):
    placed = (
        P(None, ("energy", "slab"), None, ("col", "orb")),
        P(None, ("energy", "slab"), "orb", None),
        P(None, ("energy", "slab"), None, "orb", None),
        P(None, ("energy", "slab"), "orb", None),
    )
    return jax.shard_map(
        functools.partial(per_device, mesh.shape["slab"], mesh.shape["col"]),
        mesh=mesh,
        in_specs=placed,
        out_specs=P(None, ("energy", "slab"), None, ("col", "orb")),
        check_vma=False,
    )
```
